32 devices in a mesh: wide: 8 (over y, x, core), narrow: 4 (over z).
Axes of the slice: x: 2, y: 2, z: 4, core: 2. Of those that a mesh axis runs over, the one named last changes fastest.
Arguments:
- vectors: bfloat16 [3, 4096, 128], P(None, ('wide', 'narrow')), may hold values from -18 to 18
- hessian: bfloat16 [3, 3, 61, 4096], P(None, None, None, ('wide', 'narrow')), may hold values from -0.9 to 5.4
- neighbours: int32 [60, 4096], P(None, ('wide', 'narrow')), may hold values from 0 to 415
- halo_atoms: int32 [1024], P(('wide', 'narrow')), may hold values from 0 to 127
- labels: int32 [4096], P(('wide', 'narrow')), may hold values from 0 to 15
- masses: float32 [2, 16], replicated, may hold values from 1 to 32
- rotation: float32 [2, 128, 128], replicated, may hold values from -0.5 to 0.5
Outputs:
- gram: float32 [2, 128, 128], replicated
- rotated: bfloat16 [2, 3, 4096, 128], P(None, None, ('wide', 'narrow'))
The draws below stay inside these ranges and needn't reach their ends.
Inputs may be any that keep to these rules, and one draw needn't show every extreme that they name: `neighbours`: A row below 128 is a local atom of the domain; a row r at or above it is boundary atom (r - 128) % 32 of block (r - 128) // 32 in the 3x3 order of the steps.
All inputs are finite; a program needn't handle non-finite values.
Results may differ from the reference program's by a relative error of at most 0.003.
Values may be sent and summed in bfloat16 or wider, within the bound.
No kernel may reach another device: no remote copies, remote signals or barrier semaphores. Data moves between devices by JAX's collectives and lax.ppermute only.
A program may use at most 64 MiB of HBM per device.

```python
import math
import jax
import jax.numpy as jnp
from jax import lax

NV = 128
NEIGH = 60
NISO = 16
A_DEV = 128
HALO_DEV = 32
ATOM_COUNT = 4096
HALOS = 1024
N_WIDE = 8
N_NARROW = 4


def draw_vectors(key, part):
    key_base = jax.random.fold_in(key, 11)
    key_rough = jax.random.fold_in(key, 12)
    shape = (3, ATOM_COUNT, NV)
    base = jnp.clip(jax.random.normal(key_base, shape, jnp.float32), -4.0, 4.0)
    ramp = jnp.exp(jnp.log(3.0) * jnp.arange(ATOM_COUNT, dtype=jnp.float32) / ATOM_COUNT)
    rough = jax.random.uniform(key_rough, (1, ATOM_COUNT, 1), jnp.float32, 0.5, 1.5)
    return (base * ramp[None, :, None] * rough).astype(jnp.bfloat16)


def draw_hessian(key, part):
    key_noise = jax.random.fold_in(key, 21)
    key_rough = jax.random.fold_in(key, 22)
    key_diag = jax.random.fold_in(key, 23)
    shape = (3, 3, NEIGH + 1, ATOM_COUNT)
    noise = jnp.clip(0.15 * jax.random.normal(key_noise, shape, jnp.float32), -0.6, 0.6)
    diag = jax.random.uniform(key_diag, (1, 1, 1, ATOM_COUNT), jnp.float32, 2.0, 4.0)
    rough = jax.random.uniform(key_rough, (1, 1, 1, ATOM_COUNT), jnp.float32, 0.5, 1.5)
    slot_zero = (jnp.arange(NEIGH + 1) == 0).astype(jnp.float32)[None, None, :, None]
    identity = jnp.eye(3, dtype=jnp.float32)[:, :, None, None]
    return (noise * rough + identity * slot_zero * diag).astype(jnp.bfloat16)


def set_ends(values, rng, smallest, top_value):
    shape = values.shape
    index_at = [jax.random.randint(jax.random.fold_in(rng, axis), (), 0, shape[axis]) for axis in range(len(shape))]
    values = values.at[tuple(index_at)].set(smallest)
    longest = shape.index(max(shape))
    index_at[longest] = (index_at[longest] + 1) % shape[longest]
    return values.at[tuple(index_at)].set(top_value)


def scatter_about(own_key, shape, spread, most, held_as=jnp.bfloat16):
    return jnp.clip(spread * jax.random.normal(own_key, shape, jnp.float32), -most, most).astype(held_as)


def setup_inputs(seed: int = 0) -> dict:
    key_list = jax.random.split(jax.random.key(seed), 8)
    vectors = draw_vectors(jax.random.fold_in(key_list[7], 71), 0)
    hessian = draw_hessian(jax.random.fold_in(key_list[7], 71), 0)
    neighbours = set_ends(jax.random.randint(key_list[2], (NEIGH, ATOM_COUNT), 0, A_DEV + 9 * HALO_DEV), jax.random.fold_in(key_list[2], 1), 0, (A_DEV + 9 * HALO_DEV) - 1).astype(jnp.int32)
    halo_atoms = set_ends(jax.random.randint(key_list[3], (HALOS,), 0, A_DEV), jax.random.fold_in(key_list[3], 1), 0, A_DEV - 1).astype(jnp.int32)
    labels = set_ends(jax.random.randint(key_list[4], (ATOM_COUNT,), 0, NISO), jax.random.fold_in(key_list[4], 1), 0, NISO - 1).astype(jnp.int32)
    masses = jnp.clip(jnp.exp(jax.random.uniform(key_list[5], (2, NISO), jnp.float32, math.log(1.0), math.log(32.0))), 1.0, 32.0)
    rotation = scatter_about(key_list[6], (2, NV, NV), NV ** -0.5, 0.5, jnp.float32)
    return {"vectors": vectors, "hessian": hessian, "neighbours": neighbours, "halo_atoms": halo_atoms, "labels": labels, "masses": masses, "rotation": rotation}


def reference(vectors, hessian, neighbours, halo_atoms, labels, masses, rotation):
    factors = lax.rsqrt(masses)[:, labels]
    vector_complete = vectors.astype(jnp.float32)
    scaled = jnp.concatenate([vector_complete * factors[0][None, :, None], vector_complete * factors[1][None, :, None]], axis=2).astype(jnp.bfloat16)

    def device_image(domain):
        wide_pos = domain // N_NARROW
        narrow_pos = domain % N_NARROW
        local = lax.dynamic_slice_in_dim(scaled, domain * A_DEV, A_DEV, 1)
        pieces = [local]
        for offset_a in range(3):
            for offset_b in range(3):
                src_wide = wide_pos + offset_a - 1
                src_narrow = narrow_pos + offset_b - 1
                inside = (src_wide >= 0) & (src_wide < N_WIDE) & (src_narrow >= 0) & (src_narrow < N_NARROW)
                source = (jnp.clip(src_wide, 0, N_WIDE - 1) * N_NARROW + jnp.clip(src_narrow, 0, N_NARROW - 1)).astype(jnp.int32)
                source_rows = lax.dynamic_slice_in_dim(halo_atoms, source * HALO_DEV, HALO_DEV) + source * A_DEV
                piece = jnp.take(scaled, source_rows.astype(jnp.int32), axis=1)
                pieces.append(jnp.where(inside, piece, jnp.zeros_like(piece)))
        extended = jnp.concatenate(pieces, axis=1)
        near = lax.dynamic_slice_in_dim(neighbours, domain * A_DEV, A_DEV, 1)
        blocks = lax.dynamic_slice_in_dim(hessian, domain * A_DEV, A_DEV, 3).astype(jnp.float32)
        picked = jnp.take(extended, near.reshape(-1), axis=1).reshape(3, NEIGH, A_DEV, 2 * NV).astype(jnp.float32)
        own_term = jnp.einsum('ija,jac->iac', blocks[:, :, 0], local.astype(jnp.float32), precision=lax.Precision.HIGHEST)
        far_term = jnp.einsum('ijka,jkac->iac', blocks[:, :, 1:], picked, precision=lax.Precision.HIGHEST)
        return own_term + far_term
    domains = jnp.arange(N_WIDE * N_NARROW, dtype=jnp.int32)
    images = lax.map(device_image, domains)
    product = jnp.moveaxis(images, 0, 1).reshape(3, ATOM_COUNT, 2 * NV)
    grams = []
    outputs = []
    for isotope_variant in range(2):
        hessian_image = product[:, :, isotope_variant * NV:(isotope_variant + 1) * NV] * factors[isotope_variant][None, :, None]
        gram_vector_block = jnp.einsum('eqv,eqh->vh', vector_complete, hessian_image, precision=lax.Precision.HIGHEST) / (3.0 * ATOM_COUNT)
        fresh_block = hessian_image - jnp.einsum('jyx,xs->jys', vector_complete, gram_vector_block, precision=lax.Precision.HIGHEST)
        turned_block = jnp.einsum('jyx,xs->jys', fresh_block, rotation[isotope_variant], precision=lax.Precision.HIGHEST)
        grams.append(gram_vector_block)
        outputs.append(turned_block.astype(jnp.bfloat16))
    return (jnp.stack(grams), jnp.stack(outputs))
```

```python
import jax
import jax.numpy as jnp
from jax import lax
from jax.experimental import pallas as pl
from jax.experimental.pallas import tpu as pltpu
from jax.sharding import PartitionSpec as P

AXES = ("wide", "narrow")
F32 = jnp.float32
BF16 = jnp.bfloat16
I32 = jnp.int32
VMEM = pl.BlockSpec(memory_space=pltpu.VMEM)


def iota(shape, dim):
    return lax.broadcasted_iota(I32, shape, dim)


def split(x):
    hi = x.astype(BF16)
    return hi, (x - hi.astype(F32)).astype(BF16)


def dot(a, b):
    return jnp.dot(a, b, preferred_element_type=F32)


def column(row):
    n = row.shape[1]
    return jnp.sum(jnp.where(iota((n, n), 0) == iota((n, n), 1), row, 0), axis=1, keepdims=True)


def factor_rows(labels_row, masses):
    classes = masses.shape[1]
    hit = labels_row == iota((classes, labels_row.shape[1]), 0)
    roots = lax.rsqrt(masses)
    return [
        jnp.sum(jnp.where(hit, column(roots[v : v + 1]), 0.0), axis=0, keepdims=True)
        for v in range(2)
    ]


def boundary_kernel(vectors_ref, halo_ref, labels_ref, masses_ref, out_ref):
    atoms = vectors_ref.shape[1]
    width = vectors_ref.shape[2]
    bound = halo_ref.shape[1]
    factors = factor_rows(labels_ref[...], masses_ref[...])
    picks = column(halo_ref[...]) == iota((bound, atoms), 1)
    onehot = picks.astype(F32).astype(BF16)
    cols = [jnp.sum(jnp.where(picks, f, 0.0), axis=1, keepdims=True) for f in factors]
    for j in range(3):
        rows = dot(onehot, vectors_ref[j])
        for v in range(2):
            out_ref[j, :, v * width : (v + 1) * width] = (rows * cols[v]).astype(BF16)


def build_kernel(
    vectors_ref, hessian_ref, near_ref, labels_ref, masses_ref,
    m_ref, scaled_ref, factor_ref, vt_ref,
    near_scr, ht_scr, onehot_scr,
    *, n_wide, n_narrow, bound, rows_pad,
):
    atoms = vectors_ref.shape[1]
    width = vectors_ref.shape[2]
    slots = hessian_ref.shape[2]
    kpad = near_scr.shape[0]
    group = 16
    p = lax.axis_index("wide")
    q = lax.axis_index("narrow")
    near = near_ref[...]
    rel = near - atoms
    block = jnp.zeros_like(rel)
    for b in range(1, 9):
        block = block + (rel >= b * bound).astype(I32)
    bi = (block >= 3).astype(I32) + (block >= 6).astype(I32)
    bj = block - 3 * bi
    wp, zp = p + bi - 1, q + bj - 1
    inside = (wp >= 0) & (wp < n_wide) & (zp >= 0) & (zp < n_narrow)
    even_w, even_z = lax.rem(p, 2) == 0, lax.rem(q, 2) == 0
    up_w, down_w = jnp.where(even_w, 1, 2), jnp.where(even_w, 2, 1)
    up_z, down_z = jnp.where(even_z, 1, 2), jnp.where(even_z, 2, 1)
    sw = jnp.where(bi == 1, 0, jnp.where(bi == 2, up_w, down_w))
    sz = jnp.where(bj == 1, 0, jnp.where(bj == 2, up_z, down_z))
    placed = atoms + (sw * 3 + sz) * bound + (rel - block * bound)
    near = jnp.where(rel < 0, near, jnp.where(inside, placed, -1))
    near_scr[kpad - 8 :, :] = jnp.full((8, atoms), -1, I32)
    near_scr[0:1, :] = iota((1, atoms), 1)
    near_scr[1:slots, :] = near
    for c in range(3):
        for j in range(3):
            h = hessian_ref[c, j].astype(F32)
            h = jnp.concatenate([h, jnp.zeros((kpad - slots, atoms), F32)], axis=0)
            h = jnp.concatenate([h] * (atoms // kpad), axis=0)
            ht_scr[c * 3 + j] = h.T.astype(BF16)
    own = iota((group, group * kpad), 0) == iota((group, group * kpad), 1) // kpad
    own = own.astype(F32).astype(BF16)
    per = group * kpad // atoms
    lanes = iota((kpad, rows_pad), 1)

    def body(g, carry):
        base = pl.multiple_of(g * group, group)
        turned = pltpu.roll(near_scr[...], lax.rem(atoms - base, atoms), 1)
        for a in range(group):
            hit = turned[:, a : a + 1] == lanes
            onehot_scr[a * kpad : (a + 1) * kpad, :] = hit.astype(F32).astype(BF16)
        blocks = []
        for cj in range(9):
            h = ht_scr[cj, pl.ds(base, group), :]
            blocks.append(jnp.concatenate([h] * per, axis=1) * own)
        res = dot(jnp.concatenate(blocks, axis=0), onehot_scr[...])
        hi, lo = split(res)
        for c in range(3):
            for j in range(3):
                cj = c * 3 + j
                for t, part in enumerate((hi, lo)):
                    at = pl.multiple_of((t * 3 + c) * atoms + base, group)
                    m_ref[j, pl.ds(at, group), :] = part[cj * group : (cj + 1) * group]
        return carry

    lax.fori_loop(0, atoms // group, body, 0)
    factors = factor_rows(labels_ref[...], masses_ref[...])
    for v in range(2):
        f = jnp.broadcast_to(column(factors[v]), (atoms, width))
        factor_ref[v] = f
        for j in range(3):
            scaled_ref[j, :, v * width : (v + 1) * width] = (
                vectors_ref[j].astype(F32) * f
            ).astype(BF16)
    for j in range(3):
        vt_ref[:, j * atoms : (j + 1) * atoms] = vectors_ref[j].astype(F32).T.astype(BF16)


def apply_kernel(
    m_ref, scaled_ref, factor_ref, vt_ref, own_ref, ez_ref, oz_ref, ew_ref, ow_ref,
    image_ref, mine_ref, other_ref, ext_scr,
):
    atoms = scaled_ref.shape[1]
    width = vt_ref.shape[0]
    bound = own_ref.shape[1]
    rows_pad = ext_scr.shape[1]
    for j in range(3):
        ext_scr[j, :atoms] = scaled_ref[j]
        for s, ref in enumerate((own_ref, ez_ref, oz_ref)):
            ext_scr[j, atoms + s * bound : atoms + (s + 1) * bound] = ref[j]
        for s, ref in enumerate((ew_ref, ow_ref)):
            for z in range(3):
                at = atoms + (3 * (s + 1) + z) * bound
                ext_scr[j, at : at + bound] = ref[z, j]
        used = atoms + 9 * bound
        ext_scr[j, used:] = jnp.zeros((rows_pad - used, 2 * width), BF16)
    total = dot(m_ref[0], ext_scr[0]) + dot(m_ref[1], ext_scr[1]) + dot(m_ref[2], ext_scr[2])
    total = total[: 3 * atoms] + total[3 * atoms :]
    even = lax.rem(lax.axis_index("wide"), 2) == 0
    grams = []
    for v in range(2):
        f = factor_ref[v]
        image = total[:, v * width : (v + 1) * width] * jnp.concatenate([f] * 3, axis=0)
        image_ref[v] = image
        hi, lo = split(image)
        grams.append(dot(vt_ref[...], hi) + dot(vt_ref[...], lo))
    mine_ref[...] = jnp.where(even, grams[0], grams[1])
    other_ref[...] = jnp.where(even, grams[1], grams[0])


def turn_kernel(image_ref, rotation_ref, out_ref):
    for v in range(2):
        hi, lo = split(image_ref[v])
        rhi, rlo = split(rotation_ref[v])
        out_ref[v] = dot(hi, rhi) + (dot(lo, rhi) + dot(hi, rlo))


def final_kernel(
    mine_ref, other_ref, turned_ref, vectors_ref, rotation_ref, gram_ref, out_ref, *, count
):
    atoms = vectors_ref.shape[1]
    even = lax.rem(lax.axis_index("wide"), 2) == 0
    mine, other = mine_ref[...] / count, other_ref[...] / count
    for v in range(2):
        gram = jnp.where(even, mine, other) if v == 0 else jnp.where(even, other, mine)
        gram_ref[v] = gram
        hi, lo = split(gram)
        rhi, rlo = split(rotation_ref[v])
        step = dot(hi, rhi) + (dot(lo, rhi) + dot(hi, rlo))
        shi, slo = split(step)
        for j in range(3):
            vec = vectors_ref[j]
            turned = turned_ref[v, j * atoms : (j + 1) * atoms]
            out_ref[v, j] = (turned - (dot(vec, shi) + dot(vec, slo))).astype(BF16)


def swap(array, n_wide, n_narrow, place):
    pairs = []
    for p in range(n_wide):
        for q in range(n_narrow):
            a, b = place(p, q)
            pairs.append((p * n_narrow + q, a * n_narrow + b))
    return lax.ppermute(array, AXES, pairs)


def odd_partner(i, n):
    k = i + 1 if i % 2 else i - 1
    return k if 0 <= k < n else None


def call(kernel, out, *args, scratch=(), cost=None):
    shapes = [jax.ShapeDtypeStruct(s, d) for s, d in out]
    flops, moved = cost or (1000, 1000)
    return pl.pallas_call(
        kernel,
        out_shape=shapes,
        in_specs=[VMEM] * len(args),
        out_specs=[VMEM] * len(shapes),
        scratch_shapes=list(scratch),
        compiler_params=pltpu.CompilerParams(vmem_limit_bytes=24 * 2**20),
        cost_estimate=pl.CostEstimate(flops=flops, bytes_accessed=moved, transcendentals=0),
    )(*args)


def local(vectors, hessian, neighbours, halo_atoms, labels, masses, rotation):
    n_wide = lax.axis_size("wide")
    n_narrow = lax.axis_size("narrow")
    atoms, width = vectors.shape[1:]
    bound = halo_atoms.shape[0]
    slots = hessian.shape[2]
    kpad = -(-slots // 64) * 64
    rows = atoms + 9 * bound
    rows_pad = -(-rows // 128) * 128

    def exchange(array, place):
        return swap(array, n_wide, n_narrow, place)

    def odd_z(p, q):
        k = odd_partner(q, n_narrow)
        return (p ^ 1, q) if k is None else (p, k)

    def odd_w(p, q):
        k = odd_partner(p, n_wide)
        return (p, q ^ 1) if k is None else (k, q)

    labels_row = labels.reshape(1, atoms)
    halo_row = halo_atoms.reshape(1, bound)
    (rim,) = call(
        boundary_kernel, [((3, bound, 2 * width), BF16)], vectors, halo_row, labels_row, masses
    )
    ez = exchange(rim, lambda p, q: (p, q ^ 1))
    oz = exchange(rim, odd_z)

    def build(*refs):
        build_kernel(*refs, n_wide=n_wide, n_narrow=n_narrow, bound=bound, rows_pad=rows_pad)

    m, scaled, factor, vt = call(
        build,
        [
            ((3, 6 * atoms, rows_pad), BF16),
            ((3, atoms, 2 * width), BF16),
            ((2, atoms, width), F32),
            ((width, 3 * atoms), BF16),
        ],
        vectors, hessian, neighbours, labels_row, masses,
        scratch=[
            pltpu.VMEM((kpad, atoms), I32),
            pltpu.VMEM((9, atoms, atoms), BF16),
            pltpu.VMEM((16 * kpad, rows_pad), BF16),
        ],
        cost=(2 * 9 * atoms * 16 * kpad * rows_pad, 8 * 2**20),
    )
    three = jnp.stack([rim, ez, oz])
    ew = exchange(three, lambda p, q: (p ^ 1, q))
    ow = exchange(three, odd_w)
    image, mine, other = call(
        apply_kernel,
        [((2, 3 * atoms, width), F32), ((width, width), F32), ((width, width), F32)],
        m, scaled, factor, vt, rim, ez, oz, ew, ow,
        scratch=[pltpu.VMEM((3, rows_pad, 2 * width), BF16)],
        cost=(2 * 18 * atoms * rows_pad * 2 * width, 4 * 2**20),
    )
    (turned,) = call(
        turn_kernel, [((2, 3 * atoms, width), F32)], image, rotation,
        cost=(2 * 18 * atoms * width * width, 2**20),
    )
    total = mine + exchange(other, lambda p, q: (p ^ 1, q))
    bits = [(1 << k, 0) for k in range(1, n_wide.bit_length() - 1)]
    bits += [(0, 1 << k) for k in range(n_narrow.bit_length() - 1)]
    for k in range(0, len(bits), 2):
        steps = list(bits[k : k + 2])
        if len(steps) == 2:
            steps.insert(0, (steps[0][0] ^ steps[1][0], steps[0][1] ^ steps[1][1]))
        parts = [exchange(total, lambda p, q, s=s: (p ^ s[0], q ^ s[1])) for s in steps]
        for part in parts:
            total = total + part
    other = exchange(total, lambda p, q: (p ^ 1, q))
    count = 3.0 * atoms * n_wide * n_narrow

    def final(*refs):
        final_kernel(*refs, count=count)

    gram, rotated = call(
        final,
        [((2, width, width), F32), ((2, 3, atoms, width), BF16)],
        total, other, turned, vectors, rotation,
    )
    return gram, rotated


def solution(mesh):
    for size in mesh.shape.values():
        assert size & (size - 1) == 0 and size > 1
    return jax.shard_map(
        local,
        mesh=mesh,
        in_specs=(
            P(None, AXES, None),
            P(None, None, None, AXES),
            P(None, AXES),
            P(AXES),
            P(AXES),
            P(),
            P(),
        ),
        out_specs=(P(), P(None, None, AXES, None)),
        check_vma=False,
    )
```

```python
import jax
import jax.numpy as jnp
from jax import lax
from jax.experimental import pallas as pl
from jax.experimental.pallas import tpu as pltpu
from jax.sharding import PartitionSpec as P

AXES = ("wide", "narrow")
F32 = jnp.float32
BF16 = jnp.bfloat16
I32 = jnp.int32
VMEM = pl.BlockSpec(memory_space=pltpu.VMEM)


def iota(shape, dim):
    return lax.broadcasted_iota(I32, shape, dim)


def split(x):
    hi = x.astype(BF16)
    return hi, (x - hi.astype(F32)).astype(BF16)


def dot(a, b):
    return jnp.dot(a, b, preferred_element_type=F32)


def column(row):
    n = row.shape[1]
    return jnp.sum(jnp.where(iota((n, n), 0) == iota((n, n), 1), row, 0), axis=1, keepdims=True)


def factor_rows(labels_row, masses):
    classes = masses.shape[1]
    hit = labels_row == iota((classes, labels_row.shape[1]), 0)
    roots = lax.rsqrt(masses)
    return [
        jnp.sum(jnp.where(hit, column(roots[v : v + 1]), 0.0), axis=0, keepdims=True)
        for v in range(2)
    ]


def prepare_kernel(
    vectors_hbm, halo_hbm, labels_hbm, masses_hbm, near_hbm, hessian_hbm, rotation_hbm,
    rim_ref, vectors_ref, labels_ref, masses_ref, near_ref, hessian_ref, rotation_ref,
    halo_ref, sems,
):
    pairs = (
        (vectors_hbm, vectors_ref), (halo_hbm, halo_ref), (labels_hbm, labels_ref),
        (masses_hbm, masses_ref), (near_hbm, near_ref), (hessian_hbm, hessian_ref),
        (rotation_hbm, rotation_ref),
    )
    copies = [pltpu.make_async_copy(a, b, sems.at[i]) for i, (a, b) in enumerate(pairs)]
    for copy in copies:
        copy.start()
    for copy in copies[:4]:
        copy.wait()
    atoms, width = vectors_ref.shape[1:]
    bound = halo_ref.shape[1]
    factors = factor_rows(labels_ref[...], masses_ref[...])
    picks = column(halo_ref[...]) == iota((bound, atoms), 1)
    onehot = picks.astype(F32).astype(BF16)
    for j in range(3):
        rim_ref[j] = dot(onehot, vectors_ref[j]).astype(BF16)
    lane = iota((bound, width), 1)
    packed = jnp.zeros((bound, width), F32)
    for v in range(2):
        rest = jnp.sum(jnp.where(picks, factors[v], 0.0), axis=1, keepdims=True)
        for k in range(3):
            part = rest.astype(BF16).astype(F32)
            packed = jnp.where(lane == 3 * v + k, part, packed)
            rest = rest - part
    rim_ref[3] = packed.astype(BF16)
    for copy in copies[4:]:
        copy.wait()


def scale_rows(blocks, ext_ref, base):
    bound, width = blocks[0].shape[1:]
    count = bound * len(blocks)
    shape = (width, 2 * width)
    spread = (iota(shape, 0) // 3 == iota(shape, 1) // width).astype(F32).astype(BF16)
    factor = dot(jnp.concatenate([b[3] for b in blocks], axis=0), spread)
    for j in range(3):
        rows = jnp.concatenate([b[j] for b in blocks], axis=0).astype(F32)
        rows = jnp.concatenate([rows, rows], axis=1) * factor
        ext_ref[j, base : base + count] = rows.astype(BF16)


def one_group(near, ht_ref, onehot_scr, store, g, group):
    kpad, atoms = near.shape
    lanes = iota((kpad, onehot_scr.shape[1]), 1)
    shape = (group, group * kpad)
    own = (iota(shape, 0) == iota(shape, 1) // kpad).astype(F32).astype(BF16)
    per = group * kpad // atoms
    for a in range(group):
        at = g * group + a
        hit = near[:, at : at + 1] == lanes
        onehot_scr[a * kpad : (a + 1) * kpad, :] = hit.astype(F32).astype(BF16)
    blocks = []
    for cj in range(9):
        h = ht_ref[cj, g * group : (g + 1) * group, :]
        blocks.append(jnp.concatenate([h] * per, axis=1) * own)
    res = dot(jnp.concatenate(blocks, axis=0), onehot_scr[...])
    for cj in range(9):
        hi, lo = split(res[cj * group : (cj + 1) * group])
        store(cj // 3, cj % 3, hi, lo)


def first_kernel(
    near_in, hessian_ref, m_ref, near_ref, ht_ref, onehot_scr, *, n_wide, n_narrow, bound, w_base
):
    atoms = near_in.shape[1]
    slots = hessian_ref.shape[2]
    kpad = near_ref.shape[0]
    group = 16
    p = lax.axis_index("wide")
    q = lax.axis_index("narrow")
    near = near_in[...]
    rel = near - atoms
    block = jnp.zeros_like(rel)
    for b in range(1, 9):
        block = block + (rel >= b * bound).astype(I32)
    bi = (block >= 3).astype(I32) + (block >= 6).astype(I32)
    bj = block - 3 * bi
    wp, zp = p + bi - 1, q + bj - 1
    inside = (wp >= 0) & (wp < n_wide) & (zp >= 0) & (zp < n_narrow)
    even_w, even_z = lax.rem(p, 2) == 0, lax.rem(q, 2) == 0
    up_w, down_w = jnp.where(even_w, 1, 2), jnp.where(even_w, 2, 1)
    up_z, down_z = jnp.where(even_z, 1, 2), jnp.where(even_z, 2, 1)
    sw = jnp.where(bi == 1, 0, jnp.where(bi == 2, up_w, down_w))
    sz = jnp.where(bj == 1, 0, jnp.where(bj == 2, up_z, down_z))
    head = jnp.where(sw == 0, atoms, w_base + (sw - 1) * 3 * bound)
    placed = head + sz * bound + (rel - block * bound)
    near = jnp.where(rel < 0, near, jnp.where(inside, placed, -1))
    near_ref[kpad - 8 :, :] = jnp.full((8, atoms), -1, I32)
    near_ref[0:1, :] = iota((1, atoms), 1)
    near_ref[1:slots, :] = near
    for c in range(3):
        for j in range(3):
            h = hessian_ref[c, j].astype(F32)
            h = jnp.concatenate([h, jnp.zeros((kpad - slots, atoms), F32)], axis=0)
            h = jnp.concatenate([h] * (atoms // kpad), axis=0)
            ht_ref[c * 3 + j] = h.T.astype(BF16)
    half = atoms // 2
    near = near_ref[...]
    for g in range(half // group):

        def store(c, j, hi, lo, g=g):
            for t, part in enumerate((hi, lo)):
                at = (t * 3 + c) * half + g * group
                m_ref[j, at : at + group, :] = part

        one_group(near, ht_ref, onehot_scr, store, g, group)


def second_kernel(
    m1_ref, near_ref, ht_ref, vectors_ref, labels_ref, masses_ref, rim_ref, ez_ref, oz_ref,
    m2_ref, product_ref, factor_ref, vt_ref,
    onehot_scr, local_scr, ext_scr,
):
    atoms, width = vectors_ref.shape[1:]
    bound = rim_ref.shape[1]
    w_base = ext_scr.shape[1]
    half = atoms // 2
    group = 16
    near = near_ref[...]
    for g in range(half // group):

        def store(c, j, hi, lo, g=g):
            for t, part in enumerate((hi, lo)):
                at = (t * 3 + c) * half + g * group
                local_scr[j, at : at + group, :] = part[:, :w_base]
                m2_ref[j, at : at + group, :] = part[:, w_base:]

        one_group(near, ht_ref, onehot_scr, store, g + half // group, group)
    factors = factor_rows(labels_ref[...], masses_ref[...])
    for v in range(2):
        f = jnp.broadcast_to(column(factors[v]), (atoms, width))
        factor_ref[v] = f
        for j in range(3):
            rows = vectors_ref[j].astype(F32) * f
            ext_scr[j, :atoms, v * width : (v + 1) * width] = rows.astype(BF16)
    scale_rows([rim_ref, ez_ref, oz_ref], ext_scr, atoms)
    used = atoms + 3 * bound
    for j in range(3):
        ext_scr[j, used:] = jnp.zeros((w_base - used, 2 * width), BF16)
        vt_ref[:, j * atoms : (j + 1) * atoms] = vectors_ref[j].astype(F32).T.astype(BF16)
    for h in range(2):
        total = 0.0
        for j in range(3):
            m = m1_ref[j, :, :w_base] if h == 0 else local_scr[j]
            total = total + dot(m, ext_scr[j])
        product_ref[h] = total[: 3 * half] + total[3 * half :]


def apply_kernel(
    m1_ref, m2_ref, product_ref, factor_ref, vt_ref, ew_ref, ow_ref,
    image_ref, mine_ref, other_ref, ext_scr,
):
    width, rows = vt_ref.shape
    atoms = rows // 3
    half = atoms // 2
    bound = ew_ref.shape[2]
    w_base = m1_ref.shape[2] - ext_scr.shape[1]
    scale_rows([ref.at[z] for ref in (ew_ref, ow_ref) for z in range(3)], ext_scr, 0)
    used = 6 * bound
    if used < ext_scr.shape[1]:
        for j in range(3):
            ext_scr[j, used:] = jnp.zeros((ext_scr.shape[1] - used, 2 * width), BF16)
    products = []
    for h in range(2):
        total = 0.0
        for j in range(3):
            m = m1_ref[j, :, w_base:] if h == 0 else m2_ref[j]
            total = total + dot(m, ext_scr[j])
        products.append(product_ref[h] + (total[: 3 * half] + total[3 * half :]))
    even = lax.rem(lax.axis_index("wide"), 2) == 0
    grams = []
    for v in range(2):
        parts = []
        for c in range(3):
            for h in range(2):
                block = products[h][c * half : (c + 1) * half, v * width : (v + 1) * width]
                parts.append(block * factor_ref[v, h * half : (h + 1) * half])
        image = jnp.concatenate(parts, axis=0)
        image_ref[v] = image
        hi, lo = split(image)
        grams.append(dot(vt_ref[...], hi) + dot(vt_ref[...], lo))
    mine_ref[...] = jnp.where(even, grams[0], grams[1])
    other_ref[...] = jnp.where(even, grams[1], grams[0])


def turn_kernel(image_ref, rotation_ref, out_ref):
    for v in range(2):
        hi, lo = split(image_ref[v])
        rhi, rlo = split(rotation_ref[v])
        out_ref[v] = dot(hi, rhi) + (dot(lo, rhi) + dot(hi, rlo))


def final_kernel(
    mine_ref, other_ref, turned_ref, vectors_ref, rotation_ref, gram_ref, out_ref, *, count
):
    atoms = vectors_ref.shape[1]
    even = lax.rem(lax.axis_index("wide"), 2) == 0
    mine, other = mine_ref[...] / count, other_ref[...] / count
    for v in range(2):
        gram = jnp.where(even, mine, other) if v == 0 else jnp.where(even, other, mine)
        gram_ref[v] = gram
        hi, lo = split(gram)
        rhi, rlo = split(rotation_ref[v])
        step = dot(hi, rhi) + (dot(lo, rhi) + dot(hi, rlo))
        shi, slo = split(step)
        for j in range(3):
            vec = vectors_ref[j]
            turned = turned_ref[v, j * atoms : (j + 1) * atoms]
            out_ref[v, j] = (turned - (dot(vec, shi) + dot(vec, slo))).astype(BF16)


def swap(array, n_wide, n_narrow, place):
    pairs = []
    for p in range(n_wide):
        for q in range(n_narrow):
            a, b = place(p, q)
            pairs.append((p * n_narrow + q, a * n_narrow + b))
    return lax.ppermute(array, AXES, pairs)


def odd_partner(i, n):
    k = i + 1 if i % 2 else i - 1
    return k if 0 <= k < n else None


def call(kernel, out, *args, scratch=(), cost=None, space=VMEM):
    shapes = [jax.ShapeDtypeStruct(s, d) for s, d in out]
    flops, moved = cost or (1000, 1000)
    return pl.pallas_call(
        kernel,
        out_shape=shapes,
        in_specs=[space] * len(args),
        out_specs=[VMEM] * len(shapes),
        scratch_shapes=list(scratch),
        compiler_params=pltpu.CompilerParams(vmem_limit_bytes=24 * 2**20),
        cost_estimate=pl.CostEstimate(flops=flops, bytes_accessed=moved, transcendentals=0),
    )(*args)


def local(vectors, hessian, neighbours, halo_atoms, labels, masses, rotation):
    n_wide = lax.axis_size("wide")
    n_narrow = lax.axis_size("narrow")
    atoms, width = vectors.shape[1:]
    bound = halo_atoms.shape[0]
    slots = hessian.shape[2]
    kpad = -(-slots // 64) * 64
    w_base = -(-(atoms + 3 * bound) // 128) * 128
    w_rows = -(-6 * bound // 128) * 128

    def exchange(array, place):
        return swap(array, n_wide, n_narrow, place)

    def odd_z(p, q):
        k = odd_partner(q, n_narrow)
        return (p ^ 1, q) if k is None else (p, k)

    def odd_w(p, q):
        k = odd_partner(p, n_wide)
        return (p, q ^ 1) if k is None else (k, q)

    raw = (
        vectors, halo_atoms.reshape(1, bound), labels.reshape(1, atoms), masses, neighbours,
        hessian, rotation,
    )
    raw = [pltpu.with_memory_space_constraint(a, pltpu.HBM) for a in raw]
    rim, vectors, labels, masses, near, hessian, rotation = call(
        prepare_kernel,
        [((4, bound, width), BF16)] + [(a.shape, a.dtype) for i, a in enumerate(raw) if i != 1],
        *raw,
        scratch=[pltpu.VMEM((1, bound), I32), pltpu.SemaphoreType.DMA((len(raw),))],
        space=pl.BlockSpec(memory_space=pltpu.HBM),
    )
    ez = exchange(rim, lambda p, q: (p, q ^ 1))
    oz = exchange(rim, odd_z)

    def first(*refs):
        first_kernel(*refs, n_wide=n_wide, n_narrow=n_narrow, bound=bound, w_base=w_base)

    cost = (9 * atoms * 16 * kpad * (w_base + w_rows), 4 * 2**20)
    onehot_scr = pltpu.VMEM((16 * kpad, w_base + w_rows), BF16)
    m1, near, ht = call(
        first,
        [
            ((3, 3 * atoms, w_base + w_rows), BF16),
            ((kpad, atoms), I32),
            ((9, atoms, atoms), BF16),
        ],
        near, hessian, scratch=[onehot_scr], cost=cost,
    )
    ez, oz, m1 = lax.optimization_barrier((ez, oz, m1))
    three = jnp.stack([rim, ez, oz])
    ew = exchange(three, lambda p, q: (p ^ 1, q))
    ow = exchange(three, odd_w)
    m2, product, factor, vt = call(
        second_kernel,
        [
            ((3, 3 * atoms, w_rows), BF16),
            ((2, 3 * atoms // 2, 2 * width), F32),
            ((2, atoms, width), F32),
            ((width, 3 * atoms), BF16),
        ],
        m1, near, ht, vectors, labels, masses, rim, ez, oz,
        scratch=[
            onehot_scr,
            pltpu.VMEM((3, 3 * atoms, w_base), BF16),
            pltpu.VMEM((3, w_base, 2 * width), BF16),
        ],
        cost=cost,
    )
    image, mine, other = call(
        apply_kernel,
        [((2, 3 * atoms, width), F32), ((width, width), F32), ((width, width), F32)],
        m1, m2, product, factor, vt, ew, ow,
        scratch=[pltpu.VMEM((3, w_rows, 2 * width), BF16)],
        cost=(2 * 18 * atoms * w_rows * 2 * width, 4 * 2**20),
    )
    (turned,) = call(
        turn_kernel, [((2, 3 * atoms, width), F32)], image, rotation,
        cost=(2 * 18 * atoms * width * width, 2**20),
    )
    total = mine + exchange(other, lambda p, q: (p ^ 1, q))
    bits = [(1 << k, 0) for k in range(1, n_wide.bit_length() - 1)]
    bits += [(0, 1 << k) for k in range(n_narrow.bit_length() - 1)]
    for k in range(0, len(bits), 2):
        steps = list(bits[k : k + 2])
        if len(steps) == 2:
            steps.insert(0, (steps[0][0] ^ steps[1][0], steps[0][1] ^ steps[1][1]))
        parts = [exchange(total, lambda p, q, s=s: (p ^ s[0], q ^ s[1])) for s in steps]
        for part in parts:
            total = total + part
    other = exchange(total, lambda p, q: (p ^ 1, q))
    count = 3.0 * atoms * n_wide * n_narrow

    def final(*refs):
        final_kernel(*refs, count=count)

    gram, rotated = call(
        final,
        [((2, width, width), F32), ((2, 3, atoms, width), BF16)],
        total, other, turned, vectors, rotation,
    )
    return gram, rotated


def solution(mesh):
    for size in mesh.shape.values():
        assert size & (size - 1) == 0 and size > 1
    return jax.shard_map(
        local,
        mesh=mesh,
        in_specs=(
            P(None, AXES, None),
            P(None, None, None, AXES),
            P(None, AXES),
            P(AXES),
            P(AXES),
            P(),
            P(),
        ),
        out_specs=(P(), P(None, None, AXES, None)),
        check_vma=False,
    )
```

```python
import functools

import jax
import jax.numpy as jnp
from jax import lax
from jax.experimental import pallas as pl
from jax.experimental.pallas import tpu as pltpu
from jax.sharding import PartitionSpec as P

AXES = ("wide", "narrow")
F32 = jnp.float32
BF16 = jnp.bfloat16
I32 = jnp.int32
VMEM = pl.BlockSpec(memory_space=pltpu.VMEM)


def iota(shape, dim):
    return lax.broadcasted_iota(I32, shape, dim)


def split(x):
    hi = x.astype(BF16)
    return hi, (x - hi.astype(F32)).astype(BF16)


def dot(a, b):
    return jnp.dot(a, b, preferred_element_type=F32)


def column(row):
    n = row.shape[1]
    return jnp.sum(jnp.where(iota((n, n), 0) == iota((n, n), 1), row, 0), axis=1, keepdims=True)


def factor_rows(labels_row, masses):
    classes = masses.shape[1]
    hit = labels_row == iota((classes, labels_row.shape[1]), 0)
    roots = lax.rsqrt(masses)
    return [
        jnp.sum(jnp.where(hit, column(roots[v : v + 1]), 0.0), axis=0, keepdims=True)
        for v in range(2)
    ]


def prepare_kernel(
    vectors_hbm, halo_hbm, labels_hbm, masses_hbm, near_hbm, hessian_hbm, rotation_hbm,
    rim_ref, vectors_ref, labels_ref, masses_ref, near_ref, hessian_ref, rotation_ref,
    halo_ref, sems,
):
    pairs = (
        (vectors_hbm, vectors_ref), (halo_hbm, halo_ref), (labels_hbm, labels_ref),
        (masses_hbm, masses_ref), (near_hbm, near_ref), (hessian_hbm, hessian_ref),
        (rotation_hbm, rotation_ref),
    )
    copies = [pltpu.make_async_copy(a, b, sems.at[i]) for i, (a, b) in enumerate(pairs)]
    for copy in copies:
        copy.start()
    for copy in copies[:4]:
        copy.wait()
    atoms, width = vectors_ref.shape[1:]
    bound = halo_ref.shape[1]
    factors = factor_rows(labels_ref[...], masses_ref[...])
    picks = column(halo_ref[...]) == iota((bound, atoms), 1)
    onehot = picks.astype(F32).astype(BF16)
    for j in range(3):
        rim_ref[j] = dot(onehot, vectors_ref[j]).astype(BF16)
    lane = iota((bound, width), 1)
    packed = jnp.zeros((bound, width), F32)
    for v in range(2):
        rest = jnp.sum(jnp.where(picks, factors[v], 0.0), axis=1, keepdims=True)
        for k in range(3):
            part = rest.astype(BF16).astype(F32)
            packed = jnp.where(lane == 3 * v + k, part, packed)
            rest = rest - part
    rim_ref[3] = packed.astype(BF16)
    for copy in copies[4:]:
        copy.wait()


def scale_rows(blocks, exts, base):
    bound, width = blocks[0].shape[1:]
    count = bound * len(blocks)
    shape = (width, 2 * width)
    spread = (iota(shape, 0) // 3 == iota(shape, 1) // width).astype(F32).astype(BF16)
    factor = dot(jnp.concatenate([b[3] for b in blocks], axis=0), spread)
    for j in range(3):
        rows = jnp.concatenate([b[j] for b in blocks], axis=0).astype(F32)
        rows = jnp.concatenate([rows, rows], axis=1) * factor
        exts[j][base : base + count] = rows.astype(BF16)


def one_group(near, ht_ref, onehot_scr, store, g, group):
    kpad, atoms = near.shape
    lanes = iota((kpad, onehot_scr.shape[1]), 1)
    shape = (group, group * kpad)
    own = (iota(shape, 0) == iota(shape, 1) // kpad).astype(F32).astype(BF16)
    per = group * kpad // atoms
    for a in range(group):
        at = g * group + a
        hit = near[:, at : at + 1] == lanes
        onehot_scr[a * kpad : (a + 1) * kpad, :] = hit.astype(F32).astype(BF16)
    blocks = []
    for cj in range(9):
        h = ht_ref[cj, g * group : (g + 1) * group, :]
        blocks.append(jnp.concatenate([h] * per, axis=1) * own)
    res = dot(jnp.concatenate(blocks, axis=0), onehot_scr[...])
    for cj in range(9):
        hi, lo = split(res[cj * group : (cj + 1) * group])
        store(cj // 3, cj % 3, hi, lo)


def first_kernel(
    near_in, hessian_ref, m_ref, near_ref, ht_ref, onehot_scr, *, n_wide, n_narrow, bound, w_base
):
    atoms = near_in.shape[1]
    slots = hessian_ref.shape[2]
    kpad = near_ref.shape[0]
    group = 16
    p = lax.axis_index("wide")
    q = lax.axis_index("narrow")
    near = near_in[...]
    rel = near - atoms
    block = jnp.zeros_like(rel)
    for b in range(1, 9):
        block = block + (rel >= b * bound).astype(I32)
    bi = (block >= 3).astype(I32) + (block >= 6).astype(I32)
    bj = block - 3 * bi
    wp, zp = p + bi - 1, q + bj - 1
    inside = (wp >= 0) & (wp < n_wide) & (zp >= 0) & (zp < n_narrow)
    even_w, even_z = lax.rem(p, 2) == 0, lax.rem(q, 2) == 0
    up_w, down_w = jnp.where(even_w, 1, 2), jnp.where(even_w, 2, 1)
    up_z, down_z = jnp.where(even_z, 1, 2), jnp.where(even_z, 2, 1)
    sw = jnp.where(bi == 1, 0, jnp.where(bi == 2, up_w, down_w))
    sz = jnp.where(bj == 1, 0, jnp.where(bj == 2, up_z, down_z))
    head = jnp.where(sw == 0, atoms, w_base + (sw - 1) * 3 * bound)
    placed = head + sz * bound + (rel - block * bound)
    near = jnp.where(rel < 0, near, jnp.where(inside, placed, -1))
    near_ref[kpad - 8 :, :] = jnp.full((8, atoms), -1, I32)
    near_ref[0:1, :] = iota((1, atoms), 1)
    near_ref[1:slots, :] = near
    for c in range(3):
        for j in range(3):
            h = hessian_ref[c, j].astype(F32)
            h = jnp.concatenate([h, jnp.zeros((kpad - slots, atoms), F32)], axis=0)
            h = jnp.concatenate([h] * (atoms // kpad), axis=0)
            ht_ref[c * 3 + j] = h.T.astype(BF16)
    half = atoms // 2
    near = near_ref[...]
    for g in range(half // group):

        def store(c, j, hi, lo, g=g):
            for t, part in enumerate((hi, lo)):
                at = (t * 3 + c) * half + g * group
                m_ref[j, at : at + group, :] = part

        one_group(near, ht_ref, onehot_scr, store, g, group)


def scaled_image(products, factor_ref, v):
    half = products[0].shape[0] // 3
    width = products[0].shape[1] // 2
    parts = []
    for h in range(2):
        for c in range(3):
            block = products[h][c * half : (c + 1) * half, v * width : (v + 1) * width]
            parts.append(block * factor_ref[v, h * half : (h + 1) * half])
    return jnp.concatenate(parts, axis=0)


def second_kernel(
    m1_ref, near_ref, ht_ref, vectors_ref, labels_ref, masses_ref, rim_ref, ez_ref, oz_ref,
    m2_ref, product_ref, factor_ref, gram_ref, reach_ref,
    onehot_scr, local_scr, ext_scr, vt_scr,
):
    atoms, width = vectors_ref.shape[1:]
    bound = rim_ref.shape[1]
    w_base = ext_scr.shape[1]
    half = atoms // 2
    group = 16
    near = near_ref[...]
    for g in range(half // group):

        def store(c, j, hi, lo, g=g):
            for t, part in enumerate((hi, lo)):
                at = (t * 3 + c) * half + g * group
                local_scr[j, at : at + group, :] = part[:, :w_base]
                m2_ref[j, at : at + group, :] = part[:, w_base:]

        one_group(near, ht_ref, onehot_scr, store, g + half // group, group)
    factors = factor_rows(labels_ref[...], masses_ref[...])
    for v in range(2):
        f = jnp.broadcast_to(column(factors[v]), (atoms, width))
        factor_ref[v] = f
        for j in range(3):
            rows = vectors_ref[j].astype(F32) * f
            ext_scr[j, :atoms, v * width : (v + 1) * width] = rows.astype(BF16)
    scale_rows([rim_ref, ez_ref, oz_ref], [ext_scr.at[j] for j in range(3)], atoms)
    used = atoms + 3 * bound
    for j in range(3):
        ext_scr[j, used:] = jnp.zeros((w_base - used, 2 * width), BF16)
        turned = vectors_ref[j].astype(F32).T
        for h in range(2):
            at = (3 * h + j) * half
            vt_scr[:, at : at + half] = turned[:, h * half : (h + 1) * half]
    products = []
    for h in range(2):
        total = 0.0
        for j in range(3):
            m = m1_ref[j, :, :w_base] if h == 0 else local_scr[j]
            total = total + dot(m, ext_scr[j])
        products.append(total[: 3 * half] + total[3 * half :])
        product_ref[h] = products[h]
    vt = vt_scr[...]
    for v in range(2):
        hi, lo = split(scaled_image(products, factor_ref, v))
        both = dot(vt.astype(BF16), jnp.concatenate([hi, lo], axis=1))
        gram_ref[v] = both[:, :width] + both[:, width:]
    scaled = []
    for v in range(2):
        row = factors[v]
        cols = [row[:, h * half : (h + 1) * half] for h in range(2) for c in range(3)]
        scaled.append(vt * jnp.concatenate(cols, axis=1))
    fhi, flo = split(jnp.concatenate(scaled, axis=0))
    for j in range(3):
        total = 0.0
        for h in range(2):
            at = slice(3 * h * half, 3 * (h + 1) * half)
            left = jnp.concatenate([fhi[:, at], flo[:, at]], axis=0)
            m = m1_ref[j, :, w_base:] if h == 0 else m2_ref[j]
            high = dot(left, m[: 3 * half])
            low = dot(fhi[:, at], m[3 * half :])
            total = total + (high[: 2 * width] + (high[2 * width :] + low))
        cols = total.shape[1]
        hi, lo = split(total)
        for v in range(2):
            rows = slice(v * width, (v + 1) * width)
            reach_ref[v, :, j * cols : (j + 1) * cols] = hi[rows]
            reach_ref[v, :, (3 + j) * cols : (4 + j) * cols] = lo[rows]


def partial_kernel(reach_ref, gram_ref, ew_ref, ow_ref, mine_ref, other_ref, ext_ref):
    bound, width = ew_ref.shape[2:]
    rows = ext_ref.shape[0] // 3
    used = 6 * bound
    blocks = [ref.at[z] for ref in (ew_ref, ow_ref) for z in range(3)]
    scale_rows(blocks, [ext_ref.at[j * rows : (j + 1) * rows] for j in range(3)], 0)
    if used < rows:
        for j in range(3):
            ext_ref[j * rows + used : (j + 1) * rows] = jnp.zeros((rows - used, 2 * width), BF16)
    even = lax.rem(lax.axis_index("wide"), 2) == 0
    grams = []
    for v in range(2):
        ext = ext_ref[:, v * width : (v + 1) * width]
        hi, lo = reach_ref[v, :, : 3 * rows], reach_ref[v, :, 3 * rows :]
        grams.append(gram_ref[v] + (dot(hi, ext) + dot(lo, ext)))
    mine_ref[...] = jnp.where(even, grams[0], grams[1])
    other_ref[...] = jnp.where(even, grams[1], grams[0])


def turn_kernel(m1_ref, m2_ref, product_ref, factor_ref, ext_ref, rotation_ref, out_ref):
    half = factor_ref.shape[1] // 2
    width = factor_ref.shape[2]
    rows = ext_ref.shape[0] // 3
    w_base = m1_ref.shape[2] - rows
    products = []
    for h in range(2):
        total = 0.0
        for j in range(3):
            m = m1_ref[j, :, w_base:] if h == 0 else m2_ref[j]
            total = total + dot(m, ext_ref[j * rows : (j + 1) * rows])
        products.append(product_ref[h] + (total[: 3 * half] + total[3 * half :]))
    for v in range(2):
        hi, lo = split(scaled_image(products, factor_ref, v))
        rhi, rlo = split(rotation_ref[v])
        both = dot(hi, jnp.concatenate([rhi, rlo], axis=1))
        res = both[:, :width] + (both[:, width:] + dot(lo, rhi))
        for h in range(2):
            for c in range(3):
                at = (2 * c + h) * half
                out_ref[v, at : at + half] = res[(3 * h + c) * half : (3 * h + c + 1) * half]


def finish_kernel(
    total_ref, turned_ref, vectors_ref, rotation_ref, *refs, count, own
):
    gram_hbm, out_hbm, gram_scr, out_scr, sems = refs[-5:]
    atoms = vectors_ref.shape[1]
    v = lax.rem(lax.axis_index("wide"), 2)
    v = v if own else 1 - v
    gram = total_ref[...] / count
    gram_scr[...] = gram
    first = pltpu.make_async_copy(gram_scr, gram_hbm.at[v], sems.at[0])
    first.start()
    hi, lo = split(gram)
    rhi, rlo = split(rotation_ref[v])
    step = dot(hi, rhi) + (dot(lo, rhi) + dot(hi, rlo))
    shi, slo = split(step)
    for j in range(3):
        vec = vectors_ref[j]
        turned = turned_ref[v, j * atoms : (j + 1) * atoms]
        out_scr[j] = (turned - (dot(vec, shi) + dot(vec, slo))).astype(BF16)
    second = pltpu.make_async_copy(out_scr, out_hbm.at[v], sems.at[1])
    second.start()
    first.wait()
    second.wait()


def swap(array, n_wide, n_narrow, place):
    pairs = []
    for p in range(n_wide):
        for q in range(n_narrow):
            a, b = place(p, q)
            pairs.append((p * n_narrow + q, a * n_narrow + b))
    return lax.ppermute(array, AXES, pairs)


def odd_partner(i, n):
    k = i + 1 if i % 2 else i - 1
    return k if 0 <= k < n else None


def call(kernel, out, *args, scratch=(), cost=None, space=VMEM):
    shapes = [jax.ShapeDtypeStruct(s, d) for s, d in out]
    flops, moved = cost or (1000, 1000)
    return pl.pallas_call(
        kernel,
        out_shape=shapes,
        in_specs=[space] * len(args),
        out_specs=[VMEM] * len(shapes),
        scratch_shapes=list(scratch),
        compiler_params=pltpu.CompilerParams(vmem_limit_bytes=24 * 2**20),
        cost_estimate=pl.CostEstimate(flops=flops, bytes_accessed=moved, transcendentals=0),
    )(*args)


def local(vectors, hessian, neighbours, halo_atoms, labels, masses, rotation):
    n_wide = lax.axis_size("wide")
    n_narrow = lax.axis_size("narrow")
    atoms, width = vectors.shape[1:]
    bound = halo_atoms.shape[0]
    slots = hessian.shape[2]
    kpad = -(-slots // 64) * 64
    w_base = -(-(atoms + 3 * bound) // 128) * 128
    w_rows = -(-6 * bound // 128) * 128

    def exchange(array, place):
        return swap(array, n_wide, n_narrow, place)

    def odd_z(p, q):
        k = odd_partner(q, n_narrow)
        return (p ^ 1, q) if k is None else (p, k)

    def odd_w(p, q):
        k = odd_partner(p, n_wide)
        return (p, q ^ 1) if k is None else (k, q)

    raw = (
        vectors, halo_atoms.reshape(1, bound), labels.reshape(1, atoms), masses, neighbours,
        hessian, rotation,
    )
    raw = [pltpu.with_memory_space_constraint(a, pltpu.HBM) for a in raw]
    rim, vectors, labels, masses, near, hessian, rotation = call(
        prepare_kernel,
        [((4, bound, width), BF16)] + [(a.shape, a.dtype) for i, a in enumerate(raw) if i != 1],
        *raw,
        scratch=[pltpu.VMEM((1, bound), I32), pltpu.SemaphoreType.DMA((len(raw),))],
        space=pl.BlockSpec(memory_space=pltpu.HBM),
    )
    ez = exchange(rim, lambda p, q: (p, q ^ 1))
    oz = exchange(rim, odd_z)

    def first(*refs):
        first_kernel(*refs, n_wide=n_wide, n_narrow=n_narrow, bound=bound, w_base=w_base)

    cost = (9 * atoms * 16 * kpad * (w_base + w_rows), 4 * 2**20)
    onehot_scr = pltpu.VMEM((16 * kpad, w_base + w_rows), BF16)
    m1, near, ht = call(
        first,
        [
            ((3, 3 * atoms, w_base + w_rows), BF16),
            ((kpad, atoms), I32),
            ((9, atoms, atoms), BF16),
        ],
        near, hessian, scratch=[onehot_scr], cost=cost,
    )
    ez, oz, m1 = lax.optimization_barrier((ez, oz, m1))
    three = jnp.stack([rim, ez, oz])
    ew = exchange(three, lambda p, q: (p ^ 1, q))
    ow = exchange(three, odd_w)
    m2, product, factor, gram, reach = call(
        second_kernel,
        [
            ((3, 3 * atoms, w_rows), BF16),
            ((2, 3 * atoms // 2, 2 * width), F32),
            ((2, atoms, width), F32),
            ((2, width, width), F32),
            ((2, width, 6 * w_rows), BF16),
        ],
        m1, near, ht, vectors, labels, masses, rim, ez, oz,
        scratch=[
            onehot_scr,
            pltpu.VMEM((3, 3 * atoms, w_base), BF16),
            pltpu.VMEM((3, w_base, 2 * width), BF16),
            pltpu.VMEM((width, 3 * atoms), F32),
        ],
        cost=cost,
    )
    mine, other, ext = call(
        partial_kernel,
        [((width, width), F32), ((width, width), F32), ((3 * w_rows, 2 * width), BF16)],
        reach, gram, ew, ow,
        cost=(24 * width * width * w_rows, 2**20),
    )
    (turned,) = call(
        turn_kernel, [((2, 3 * atoms, width), F32)], m1, m2, product, factor, ext, rotation,
        cost=(2 * 18 * atoms * w_rows * 2 * width, 4 * 2**20),
    )
    total = mine + exchange(other, lambda p, q: (p ^ 1, q))
    bits = [(1 << k, 0) for k in range(1, n_wide.bit_length() - 1)]
    bits += [(0, 1 << k) for k in range(n_narrow.bit_length() - 1)]
    for k in range(0, len(bits), 2):
        steps = list(bits[k : k + 2])
        if len(steps) == 2:
            steps.append((steps[0][0] ^ steps[1][0], steps[0][1] ^ steps[1][1]))
        parts = [exchange(total, lambda p, q, s=s: (p ^ s[0], q ^ s[1])) for s in steps]
        for part in parts:
            total = total + part
        if k == 0:
            total, turned = lax.optimization_barrier((total, turned))
    other = exchange(total, lambda p, q: (p ^ 1, q))
    count = 3.0 * atoms * n_wide * n_narrow
    outs = [
        jax.ShapeDtypeStruct((2, width, width), F32),
        jax.ShapeDtypeStruct((2, 3, atoms, width), BF16),
    ]
    hbm = pl.BlockSpec(memory_space=pltpu.HBM)

    def finish(total, held=()):
        return pl.pallas_call(
            functools.partial(finish_kernel, count=count, own=not held),
            out_shape=outs,
            in_specs=[VMEM] * 4 + [hbm] * len(held),
            out_specs=[hbm] * 2,
            scratch_shapes=[
                pltpu.VMEM((width, width), F32),
                pltpu.VMEM((3, atoms, width), BF16),
                pltpu.SemaphoreType.DMA((2,)),
            ],
            input_output_aliases={4: 0, 5: 1} if held else {},
            compiler_params=pltpu.CompilerParams(vmem_limit_bytes=24 * 2**20),
            cost_estimate=pl.CostEstimate(flops=10**6, bytes_accessed=10**6, transcendentals=0),
        )(total, turned, vectors, rotation, *held)

    return tuple(finish(other, finish(total)))


def solution(mesh):
    for size in mesh.shape.values():
        assert size & (size - 1) == 0 and size > 1
    return jax.shard_map(
        local,
        mesh=mesh,
        in_specs=(
            P(None, AXES, None),
            P(None, None, None, AXES),
            P(None, AXES),
            P(AXES),
            P(AXES),
            P(),
            P(),
        ),
        out_specs=(P(), P(None, None, AXES, None)),
        check_vma=False,
    )
```

```python
import functools

import jax
import jax.numpy as jnp
from jax import lax
from jax.experimental import pallas as pl
from jax.experimental.pallas import tpu as pltpu
from jax.sharding import PartitionSpec as P

AXES = ("wide", "narrow")
F32 = jnp.float32
BF16 = jnp.bfloat16
I32 = jnp.int32
VMEM = pl.BlockSpec(memory_space=pltpu.VMEM)


def iota(shape, dim):
    return lax.broadcasted_iota(I32, shape, dim)


def split(x):
    hi = x.astype(BF16)
    return hi, (x - hi.astype(F32)).astype(BF16)


def dot(a, b):
    return jnp.dot(a, b, preferred_element_type=F32)


def column(row):
    n = row.shape[1]
    return jnp.sum(jnp.where(iota((n, n), 0) == iota((n, n), 1), row, 0), axis=1, keepdims=True)


def factor_rows(labels_row, masses):
    classes = masses.shape[1]
    hit = labels_row == iota((classes, labels_row.shape[1]), 0)
    roots = lax.rsqrt(masses)
    return [
        jnp.sum(jnp.where(hit, column(roots[v : v + 1]), 0.0), axis=0, keepdims=True)
        for v in range(2)
    ]


def prepare_kernel(
    vectors_hbm, halo_hbm, labels_hbm, masses_hbm, near_hbm, hessian_hbm, rotation_hbm,
    rim_ref, vectors_ref, labels_ref, masses_ref, near_ref, hessian_ref, rotation_ref,
    halo_ref, sems,
):
    pairs = [(halo_hbm, halo_ref), (labels_hbm, labels_ref), (masses_hbm, masses_ref)]
    pairs += [(vectors_hbm.at[j], vectors_ref.at[j]) for j in range(3)]
    pairs += [(near_hbm, near_ref), (hessian_hbm, hessian_ref), (rotation_hbm, rotation_ref)]
    copies = [pltpu.make_async_copy(a, b, sems.at[i]) for i, (a, b) in enumerate(pairs)]
    for copy in copies:
        copy.start()
    for copy in copies[:6]:
        copy.wait()
    atoms, width = vectors_ref.shape[1:]
    bound = halo_ref.shape[1]
    factors = factor_rows(labels_ref[...], masses_ref[...])
    picks = column(halo_ref[...]) == iota((bound, atoms), 1)
    onehot = picks.astype(F32).astype(BF16)
    for j in range(3):
        rim_ref[j * bound : (j + 1) * bound] = dot(onehot, vectors_ref[j]).astype(BF16)
    lane = iota((bound, width), 1)
    packed = jnp.zeros((bound, width), F32)
    for v in range(2):
        rest = jnp.sum(jnp.where(picks, factors[v], 0.0), axis=1, keepdims=True)
        for k in range(3):
            part = rest.astype(BF16).astype(F32)
            packed = jnp.where(lane == 3 * v + k, part, packed)
            rest = rest - part
    fold = width // (bound // 8)
    folded = packed[:8]
    for g in range(1, bound // 8):
        folded = folded + pltpu.roll(packed[8 * g : 8 * (g + 1)], g * fold, 1)
    rim_ref[3 * bound :] = folded.astype(BF16)
    for copy in copies[6:]:
        copy.wait()


def scale_rows(blocks, exts, base):
    rows, width = blocks[0].shape
    bound = (rows - 8) // 3
    count = bound * len(blocks)
    shape = (width, 2 * width)
    spread = (iota(shape, 0) // 3 == iota(shape, 1) // width).astype(F32).astype(BF16)
    fold = width // (bound // 8)
    parts = []
    for b in blocks:
        packed = b[3 * bound :].astype(F32)
        parts += [pltpu.roll(packed, (width - g * fold) % width, 1) for g in range(bound // 8)]
    factor = dot(jnp.concatenate(parts, axis=0).astype(BF16), spread)
    for j in range(3):
        part = [b[j * bound : (j + 1) * bound] for b in blocks]
        part = jnp.concatenate(part, axis=0).astype(F32)
        part = jnp.concatenate([part, part], axis=1) * factor
        exts[j][base : base + count] = part.astype(BF16)


def one_group(near, ht_ref, onehot_scr, store, g, group):
    kpad, atoms = near.shape
    lanes = iota((kpad, onehot_scr.shape[1]), 1)
    shape = (group, group * kpad)
    own = (iota(shape, 0) == iota(shape, 1) // kpad).astype(F32).astype(BF16)
    per = group * kpad // atoms
    for a in range(group):
        at = g * group + a
        hit = near[:, at : at + 1] == lanes
        onehot_scr[a * kpad : (a + 1) * kpad, :] = hit.astype(F32).astype(BF16)
    blocks = []
    for cj in range(9):
        h = ht_ref[cj, g * group : (g + 1) * group, :]
        blocks.append(jnp.concatenate([h] * per, axis=1) * own)
    res = dot(jnp.concatenate(blocks, axis=0), onehot_scr[...])
    for cj in range(9):
        hi, lo = split(res[cj * group : (cj + 1) * group])
        store(cj // 3, cj % 3, hi, lo)


def build_kernel(
    near_in, hessian_ref, m_ref, near_ref, ht_ref, onehot_scr,
    *, n_wide, n_narrow, bound, w_base, w_step,
):
    atoms = near_in.shape[1]
    slots = hessian_ref.shape[2]
    kpad = near_ref.shape[0]
    group = 16
    p = lax.axis_index("wide")
    q = lax.axis_index("narrow")
    near = near_in[...]
    rel = near - atoms
    block = jnp.zeros_like(rel)
    for b in range(1, 9):
        block = block + (rel >= b * bound).astype(I32)
    bi = (block >= 3).astype(I32) + (block >= 6).astype(I32)
    bj = block - 3 * bi
    wp, zp = p + bi - 1, q + bj - 1
    inside = (wp >= 0) & (wp < n_wide) & (zp >= 0) & (zp < n_narrow)
    even_w, even_z = lax.rem(p, 2) == 0, lax.rem(q, 2) == 0
    up_w, down_w = jnp.where(even_w, 1, 2), jnp.where(even_w, 2, 1)
    up_z, down_z = jnp.where(even_z, 1, 2), jnp.where(even_z, 2, 1)
    sw = jnp.where(bi == 1, 0, jnp.where(bi == 2, up_w, down_w))
    sz = jnp.where(bj == 1, 0, jnp.where(bj == 2, up_z, down_z))
    head = jnp.where(sw == 0, atoms, w_base + (sw - 1) * w_step)
    placed = head + sz * bound + (rel - block * bound)
    near = jnp.where(rel < 0, near, jnp.where(inside, placed, -1))
    near_ref[kpad - 8 :, :] = jnp.full((8, atoms), -1, I32)
    near_ref[0:1, :] = iota((1, atoms), 1)
    near_ref[1:slots, :] = near
    for c in range(3):
        for j in range(3):
            h = hessian_ref[c, j].astype(F32)
            h = jnp.concatenate([h, jnp.zeros((kpad - slots, atoms), F32)], axis=0)
            h = jnp.concatenate([h] * (atoms // kpad), axis=0)
            ht_ref[c * 3 + j] = h.T.astype(BF16)
    near = near_ref[...]
    for g in range(atoms // group):

        def store(c, j, hi, lo, g=g):
            for t, part in enumerate((hi, lo)):
                at = (t * 3 + c) * atoms + g * group
                m_ref[j, at : at + group, :] = part

        one_group(near, ht_ref, onehot_scr, store, g, group)


def apply_rows(m_ref, exts, at):
    total = 0.0
    for j in range(3):
        total = total + dot(m_ref[j, :, at], exts[j])
    half = total.shape[0] // 2
    return total[:half] + total[half:]


def local_kernel(
    m_ref, vectors_ref, labels_ref, masses_ref, rim_ref, ez_ref, oz_ref,
    product_ref, factor_ref, gram_ref, reach_e_ref, reach_o_ref,
    ext_scr, vt_scr,
):
    atoms, width = vectors_ref.shape[1:]
    bound = (rim_ref.shape[0] - 8) // 3
    w_base = ext_scr.shape[1]
    factors = factor_rows(labels_ref[...], masses_ref[...])
    for v in range(2):
        f = jnp.broadcast_to(column(factors[v]), (atoms, width))
        factor_ref[v] = f
        for j in range(3):
            rows = vectors_ref[j].astype(F32) * f
            ext_scr[j, :atoms, v * width : (v + 1) * width] = rows.astype(BF16)
    scale_rows([rim_ref, ez_ref, oz_ref], [ext_scr.at[j] for j in range(3)], atoms)
    used = atoms + 3 * bound
    for j in range(3):
        ext_scr[j, used:] = jnp.zeros((w_base - used, 2 * width), BF16)
        vt_scr[:, j * atoms : (j + 1) * atoms] = vectors_ref[j].astype(F32).T
    product = apply_rows(m_ref, [ext_scr[j] for j in range(3)], slice(0, w_base))
    product_ref[...] = product
    vt = vt_scr[...]
    scaled = []
    for v in range(2):
        f = jnp.concatenate([factor_ref[v]] * 3, axis=0)
        hi, lo = split(product[:, v * width : (v + 1) * width] * f)
        both = dot(vt.astype(BF16), jnp.concatenate([hi, lo], axis=1))
        gram_ref[v] = both[:, :width] + both[:, width:]
        scaled.append(vt * jnp.concatenate([factors[v]] * 3, axis=1))
    fhi, flo = split(jnp.concatenate(scaled, axis=0))
    left = jnp.concatenate([fhi, flo], axis=0)
    for j in range(3):
        high = dot(left, m_ref[j, : 3 * atoms, w_base:])
        total = high[: 2 * width] + (high[2 * width :] + dot(fhi, m_ref[j, 3 * atoms :, w_base:]))
        cols = total.shape[1] // 2
        hi, lo = split(total)
        for v in range(2):
            rows = slice(v * width, (v + 1) * width)
            for s, ref in enumerate((reach_e_ref, reach_o_ref)):
                cut = slice(s * cols, (s + 1) * cols)
                ref[v, :width, j * cols : (j + 1) * cols] = hi[rows, cut]
                ref[v, width:, j * cols : (j + 1) * cols] = lo[rows, cut]


def partial_kernel(reach_ref, gram_ref, block_ref, *outs, last):
    ext_ref = outs[-1]
    width = block_ref.shape[2]
    bound = (block_ref.shape[1] - 8) // 3
    rows = ext_ref.shape[0] // 3
    used = 3 * bound
    blocks = [block_ref.at[z] for z in range(3)]
    scale_rows(blocks, [ext_ref.at[j * rows : (j + 1) * rows] for j in range(3)], 0)
    if used < rows:
        for j in range(3):
            ext_ref[j * rows + used : (j + 1) * rows] = jnp.zeros((rows - used, 2 * width), BF16)
    grams = []
    for v in range(2):
        both = dot(reach_ref[v], ext_ref[:, v * width : (v + 1) * width])
        grams.append(gram_ref[v] + (both[:width] + both[width:]))
    if last:
        even = lax.rem(lax.axis_index("wide"), 2) == 0
        outs[0][...] = jnp.where(even, grams[0], grams[1])
        outs[1][...] = jnp.where(even, grams[1], grams[0])
    else:
        for v in range(2):
            outs[0][v] = grams[v]


def turn_kernel(m_ref, product_ref, factor_ref, ext_e_ref, ext_o_ref, rotation_ref, out_ref):
    width = factor_ref.shape[2]
    rows = ext_e_ref.shape[0] // 3
    w_base = m_ref.shape[2] - 2 * rows
    exts = []
    for j in range(3):
        part = [ref[j * rows : (j + 1) * rows] for ref in (ext_e_ref, ext_o_ref)]
        exts.append(jnp.concatenate(part, axis=0))
    product = product_ref[...] + apply_rows(m_ref, exts, slice(w_base, None))
    for v in range(2):
        f = jnp.concatenate([factor_ref[v]] * 3, axis=0)
        hi, lo = split(product[:, v * width : (v + 1) * width] * f)
        rhi, rlo = split(rotation_ref[v])
        both = dot(hi, jnp.concatenate([rhi, rlo], axis=1))
        out_ref[v] = both[:, :width] + (both[:, width:] + dot(lo, rhi))


def finish_kernel(
    total_ref, turned_ref, vectors_ref, rotation_ref, *refs, count, own
):
    gram_hbm, out_hbm, gram_scr, out_scr, sems = refs[-5:]
    atoms = vectors_ref.shape[1]
    v = lax.rem(lax.axis_index("wide"), 2)
    v = v if own else 1 - v
    gram = total_ref[...] / count
    gram_scr[...] = gram
    copies = [pltpu.make_async_copy(gram_scr, gram_hbm.at[v], sems.at[0])]
    copies[0].start()
    hi, lo = split(gram)
    rhi, rlo = split(rotation_ref[v])
    step = dot(hi, rhi) + (dot(lo, rhi) + dot(hi, rlo))
    shi, slo = split(step)
    for j in range(3):
        vec = vectors_ref[j]
        turned = turned_ref[v, j * atoms : (j + 1) * atoms]
        out_scr[j] = (turned - (dot(vec, shi) + dot(vec, slo))).astype(BF16)
        copies.append(pltpu.make_async_copy(out_scr.at[j], out_hbm.at[v, j], sems.at[1 + j]))
        copies[-1].start()
    for copy in copies:
        copy.wait()


def swap(array, n_wide, n_narrow, place):
    pairs = []
    for p in range(n_wide):
        for q in range(n_narrow):
            a, b = place(p, q)
            pairs.append((p * n_narrow + q, a * n_narrow + b))
    return lax.ppermute(array, AXES, pairs)


def sum_stages(n_wide, n_narrow):
    bits = [(1 << k, 0) for k in range(1, n_wide.bit_length() - 1)]
    bits += [(0, 1 << k) for k in range(n_narrow.bit_length() - 1)]
    stages = []
    for k in range(0, len(bits), 2):
        steps = bits[k : k + 2]
        if steps[0][0]:
            steps = steps[::-1]
        if len(steps) == 2:
            steps.insert(0, (steps[0][0] ^ steps[1][0], steps[0][1] ^ steps[1][1]))
        stages.append(steps)
    return stages


def odd_partner(i, n):
    k = i + 1 if i % 2 else i - 1
    return k if 0 <= k < n else None


def call(kernel, out, *args, scratch=(), cost=None, space=VMEM):
    shapes = [jax.ShapeDtypeStruct(s, d) for s, d in out]
    flops, moved = cost or (1000, 1000)
    return pl.pallas_call(
        kernel,
        out_shape=shapes,
        in_specs=[space] * len(args),
        out_specs=[VMEM] * len(shapes),
        scratch_shapes=list(scratch),
        compiler_params=pltpu.CompilerParams(vmem_limit_bytes=24 * 2**20),
        cost_estimate=pl.CostEstimate(flops=flops, bytes_accessed=moved, transcendentals=0),
    )(*args)


def local(vectors, hessian, neighbours, halo_atoms, labels, masses, rotation):
    n_wide = lax.axis_size("wide")
    n_narrow = lax.axis_size("narrow")
    atoms, width = vectors.shape[1:]
    bound = halo_atoms.shape[0]
    slots = hessian.shape[2]
    kpad = -(-slots // 64) * 64
    w_base = -(-(atoms + 3 * bound) // 128) * 128
    w_step = -(-3 * bound // 128) * 128
    w_rows = 2 * w_step

    def exchange(array, place):
        return swap(array, n_wide, n_narrow, place)

    def odd_z(p, q):
        k = odd_partner(q, n_narrow)
        return (p ^ 1, q) if k is None else (p, k)

    def odd_w(p, q):
        k = odd_partner(p, n_wide)
        return (p, q ^ 1) if k is None else (k, q)

    raw = (
        vectors, halo_atoms.reshape(1, bound), labels.reshape(1, atoms), masses, neighbours,
        hessian, rotation,
    )
    hbm = pl.BlockSpec(memory_space=pltpu.HBM)
    rim, vectors, labels, masses, near, hessian, rotation = call(
        prepare_kernel,
        [((3 * bound + 8, width), BF16)] + [(a.shape, a.dtype) for i, a in enumerate(raw) if i != 1],
        *[pltpu.with_memory_space_constraint(a, pltpu.HBM) for a in raw],
        scratch=[pltpu.VMEM((1, bound), I32), pltpu.SemaphoreType.DMA((9,))],
        space=hbm,
    )
    ez = exchange(rim, lambda p, q: (p, q ^ 1))
    oz = exchange(rim, odd_z)

    def build(*refs):
        build_kernel(
            *refs, n_wide=n_wide, n_narrow=n_narrow, bound=bound, w_base=w_base, w_step=w_step
        )

    cost = (9 * atoms * 16 * kpad * (w_base + w_rows), 4 * 2**20)
    (m,) = call(
        build,
        [((3, 6 * atoms, w_base + w_rows), BF16)],
        near, hessian,
        scratch=[
            pltpu.VMEM((kpad, atoms), I32),
            pltpu.VMEM((9, atoms, atoms), BF16),
            pltpu.VMEM((16 * kpad, w_base + w_rows), BF16),
        ],
        cost=cost,
    )
    ez, oz, m = lax.optimization_barrier((ez, oz, m))
    three = jnp.stack([rim, ez, oz])
    ew = exchange(three, lambda p, q: (p ^ 1, q))
    ow = exchange(three, odd_w)
    product, factor, gram, reach_e, reach_o = call(
        local_kernel,
        [
            ((3 * atoms, 2 * width), F32),
            ((2, atoms, width), F32),
            ((2, width, width), F32),
            ((2, 2 * width, 3 * w_step), BF16),
            ((2, 2 * width, 3 * w_step), BF16),
        ],
        m, vectors, labels, masses, rim, ez, oz,
        scratch=[
            pltpu.VMEM((3, w_base, 2 * width), BF16),
            pltpu.VMEM((width, 3 * atoms), F32),
        ],
        cost=cost,
    )
    cost = (12 * width * width * w_rows, 2**20)
    rows = ((3 * w_step, 2 * width), BF16)
    square = ((width, width), F32)
    gram, ext_e = call(
        functools.partial(partial_kernel, last=False),
        [((2, width, width), F32), rows], reach_e, gram, ew, cost=cost,
    )
    mine, other, ext_o = call(
        functools.partial(partial_kernel, last=True),
        [square, square, rows], reach_o, gram, ow, cost=cost,
    )
    (turned,) = call(
        turn_kernel, [((2, 3 * atoms, width), F32)], m, product, factor, ext_e, ext_o, rotation,
        cost=(2 * 18 * atoms * w_rows * 2 * width, 4 * 2**20),
    )
    total = mine + exchange(other, lambda p, q: (p ^ 1, q))
    for k, steps in enumerate(sum_stages(n_wide, n_narrow)):
        parts = [exchange(total, lambda p, q, s=s: (p ^ s[0], q ^ s[1])) for s in steps]
        for part in parts:
            total = total + part
        if k == 0:
            total, turned = lax.optimization_barrier((total, turned))
    other = exchange(total, lambda p, q: (p ^ 1, q))
    count = 3.0 * atoms * n_wide * n_narrow
    outs = [
        jax.ShapeDtypeStruct((2, width, width), F32),
        jax.ShapeDtypeStruct((2, 3, atoms, width), BF16),
    ]

    def finish(total, held=()):
        return pl.pallas_call(
            functools.partial(finish_kernel, count=count, own=not held),
            out_shape=outs,
            in_specs=[VMEM] * 4 + [hbm] * len(held),
            out_specs=[hbm] * 2,
            scratch_shapes=[
                pltpu.VMEM((width, width), F32),
                pltpu.VMEM((3, atoms, width), BF16),
                pltpu.SemaphoreType.DMA((4,)),
            ],
            input_output_aliases={4: 0, 5: 1} if held else {},
            compiler_params=pltpu.CompilerParams(vmem_limit_bytes=24 * 2**20),
            cost_estimate=pl.CostEstimate(flops=10**6, bytes_accessed=10**6, transcendentals=0),
        )(total, turned, vectors, rotation, *held)

    return tuple(finish(other, finish(total)))


def solution(mesh):
    n_wide, n_narrow = (mesh.shape[axis] for axis in AXES)
    for size in (n_wide, n_narrow):
        assert size & (size - 1) == 0 and size > 1
    return jax.shard_map(
        local,
        mesh=mesh,
        in_specs=(
            P(None, AXES, None),
            P(None, None, None, AXES),
            P(None, AXES),
            P(AXES),
            P(AXES),
            P(),
            P(),
        ),
        out_specs=(P(), P(None, None, AXES, None)),
        check_vma=False,
    )
```

```python
import functools

import jax
import jax.numpy as jnp
from jax import lax
from jax.experimental import pallas as pl
from jax.experimental.pallas import tpu as pltpu
from jax.sharding import PartitionSpec as P

AXES = ("wide", "narrow")
F32 = jnp.float32
BF16 = jnp.bfloat16
I32 = jnp.int32
VMEM = pl.BlockSpec(memory_space=pltpu.VMEM)


def iota(shape, dim):
    return lax.broadcasted_iota(I32, shape, dim)


def split(x):
    hi = x.astype(BF16)
    return hi, (x - hi.astype(F32)).astype(BF16)


def dot(a, b):
    return jnp.dot(a, b, preferred_element_type=F32)


def column(row):
    n = row.shape[1]
    return jnp.sum(jnp.where(iota((n, n), 0) == iota((n, n), 1), row, 0), axis=1, keepdims=True)


def factor_rows(labels_row, masses):
    classes = masses.shape[1]
    hit = labels_row == iota((classes, labels_row.shape[1]), 0)
    roots = lax.rsqrt(masses)
    return [
        jnp.sum(jnp.where(hit, column(roots[v : v + 1]), 0.0), axis=0, keepdims=True)
        for v in range(2)
    ]


def prepare_kernel(
    vectors_hbm, halo_hbm, labels_hbm, masses_hbm, near_hbm, hessian_hbm, rotation_hbm,
    rim_ref, vectors_ref, labels_ref, masses_ref, near_ref, hessian_ref, rotation_ref,
    halo_ref, sems,
):
    pairs = [(halo_hbm, halo_ref), (labels_hbm, labels_ref), (masses_hbm, masses_ref)]
    pairs += [(vectors_hbm.at[j], vectors_ref.at[j]) for j in range(3)]
    pairs += [(near_hbm, near_ref), (hessian_hbm, hessian_ref), (rotation_hbm, rotation_ref)]
    copies = [pltpu.make_async_copy(a, b, sems.at[i]) for i, (a, b) in enumerate(pairs)]
    for copy in copies:
        copy.start()
    for copy in copies[:6]:
        copy.wait()
    atoms, width = vectors_ref.shape[1:]
    bound = halo_ref.shape[1]
    factors = factor_rows(labels_ref[...], masses_ref[...])
    picks = column(halo_ref[...]) == iota((bound, atoms), 1)
    onehot = picks.astype(F32).astype(BF16)
    for j in range(3):
        rim_ref[j * bound : (j + 1) * bound] = dot(onehot, vectors_ref[j]).astype(BF16)
    lane = iota((bound, width), 1)
    packed = jnp.zeros((bound, width), F32)
    for v in range(2):
        rest = jnp.sum(jnp.where(picks, factors[v], 0.0), axis=1, keepdims=True)
        for k in range(3):
            part = rest.astype(BF16).astype(F32)
            packed = jnp.where(lane == 3 * v + k, part, packed)
            rest = rest - part
    fold = width // (bound // 8)
    folded = packed[:8]
    for g in range(1, bound // 8):
        folded = folded + pltpu.roll(packed[8 * g : 8 * (g + 1)], g * fold, 1)
    rim_ref[3 * bound :] = folded.astype(BF16)
    for copy in copies[6:]:
        copy.wait()


def scale_rows(blocks, exts, base):
    rows, width = blocks[0].shape
    bound = (rows - 8) // 3
    count = bound * len(blocks)
    shape = (width, 2 * width)
    spread = (iota(shape, 0) // 3 == iota(shape, 1) // width).astype(F32).astype(BF16)
    fold = width // (bound // 8)
    parts = []
    for b in blocks:
        packed = b[3 * bound :].astype(F32)
        parts += [pltpu.roll(packed, (width - g * fold) % width, 1) for g in range(bound // 8)]
    factor = dot(jnp.concatenate(parts, axis=0).astype(BF16), spread)
    for j in range(3):
        part = [b[j * bound : (j + 1) * bound] for b in blocks]
        part = jnp.concatenate(part, axis=0).astype(F32)
        part = jnp.concatenate([part, part], axis=1) * factor
        exts[j][base : base + count] = part.astype(BF16)


def one_group(near, ht_ref, onehot_scr, store, g, group):
    kpad, atoms = near.shape
    lanes = iota((kpad, onehot_scr.shape[1]), 1)
    shape = (group, group * kpad)
    own = (iota(shape, 0) == iota(shape, 1) // kpad).astype(F32).astype(BF16)
    per = group * kpad // atoms
    for a in range(group):
        at = g * group + a
        hit = near[:, at : at + 1] == lanes
        onehot_scr[a * kpad : (a + 1) * kpad, :] = hit.astype(F32).astype(BF16)
    blocks = []
    for cj in range(9):
        h = ht_ref[cj, g * group : (g + 1) * group, :]
        blocks.append(jnp.concatenate([h] * per, axis=1) * own)
    res = dot(jnp.concatenate(blocks, axis=0), onehot_scr[...])
    for cj in range(9):
        hi, lo = split(res[cj * group : (cj + 1) * group])
        store(cj // 3, cj % 3, hi, lo)


def build_kernel(
    near_in, hessian_ref, m_ref, near_ref, ht_ref, onehot_scr,
    *, n_wide, n_narrow, bound, w_base, w_step,
):
    atoms = near_in.shape[1]
    slots = hessian_ref.shape[2]
    kpad = near_ref.shape[0]
    group = 16
    p = lax.axis_index("wide")
    q = lax.axis_index("narrow")
    near = near_in[...]
    rel = near - atoms
    block = jnp.zeros_like(rel)
    for b in range(1, 9):
        block = block + (rel >= b * bound).astype(I32)
    bi = (block >= 3).astype(I32) + (block >= 6).astype(I32)
    bj = block - 3 * bi
    wp, zp = p + bi - 1, q + bj - 1
    inside = (wp >= 0) & (wp < n_wide) & (zp >= 0) & (zp < n_narrow)
    even_w, even_z = lax.rem(p, 2) == 0, lax.rem(q, 2) == 0
    up_w, down_w = jnp.where(even_w, 1, 2), jnp.where(even_w, 2, 1)
    up_z, down_z = jnp.where(even_z, 1, 2), jnp.where(even_z, 2, 1)
    sw = jnp.where(bi == 1, 0, jnp.where(bi == 2, up_w, down_w))
    sz = jnp.where(bj == 1, 0, jnp.where(bj == 2, up_z, down_z))
    head = jnp.where(sw == 0, atoms, w_base + (sw - 1) * w_step)
    placed = head + sz * bound + (rel - block * bound)
    near = jnp.where(rel < 0, near, jnp.where(inside, placed, -1))
    near_ref[kpad - 8 :, :] = jnp.full((8, atoms), -1, I32)
    near_ref[0:1, :] = iota((1, atoms), 1)
    near_ref[1:slots, :] = near
    for c in range(3):
        for j in range(3):
            h = hessian_ref[c, j].astype(F32)
            h = jnp.concatenate([h, jnp.zeros((kpad - slots, atoms), F32)], axis=0)
            h = jnp.concatenate([h] * (atoms // kpad), axis=0)
            ht_ref[c * 3 + j] = h.T.astype(BF16)
    near = near_ref[...]
    for g in range(atoms // group):

        def store(c, j, hi, lo, g=g):
            for t, part in enumerate((hi, lo)):
                at = (t * 3 + c) * atoms + g * group
                m_ref[j, at : at + group, :] = part

        one_group(near, ht_ref, onehot_scr, store, g, group)


def apply_rows(m_ref, exts, at):
    total = 0.0
    for j in range(3):
        total = total + dot(m_ref[j, :, at], exts[j])
    half = total.shape[0] // 2
    return total[:half] + total[half:]


def local_kernel(
    m_ref, vectors_ref, labels_ref, masses_ref, rim_ref, ez_ref, oz_ref,
    product_ref, factor_ref, gram_ref, reach_e_ref, reach_o_ref,
    ext_scr, vt_scr,
):
    atoms, width = vectors_ref.shape[1:]
    bound = (rim_ref.shape[0] - 8) // 3
    w_base = ext_scr.shape[1]
    factors = factor_rows(labels_ref[...], masses_ref[...])
    for v in range(2):
        f = jnp.broadcast_to(column(factors[v]), (atoms, width))
        factor_ref[v] = f
        for j in range(3):
            rows = vectors_ref[j].astype(F32) * f
            ext_scr[j, :atoms, v * width : (v + 1) * width] = rows.astype(BF16)
    scale_rows([rim_ref, ez_ref, oz_ref], [ext_scr.at[j] for j in range(3)], atoms)
    used = atoms + 3 * bound
    for j in range(3):
        ext_scr[j, used:] = jnp.zeros((w_base - used, 2 * width), BF16)
        vt_scr[:, j * atoms : (j + 1) * atoms] = vectors_ref[j].astype(F32).T
    product = apply_rows(m_ref, [ext_scr[j] for j in range(3)], slice(0, w_base))
    product_ref[...] = product
    vt = vt_scr[...]
    scaled = []
    for v in range(2):
        f = jnp.concatenate([factor_ref[v]] * 3, axis=0)
        hi, lo = split(product[:, v * width : (v + 1) * width] * f)
        both = dot(vt.astype(BF16), jnp.concatenate([hi, lo], axis=1))
        gram_ref[v] = both[:, :width] + both[:, width:]
        scaled.append(vt * jnp.concatenate([factors[v]] * 3, axis=1))
    fhi, flo = split(jnp.concatenate(scaled, axis=0))
    left = jnp.concatenate([fhi, flo], axis=0)
    for j in range(3):
        high = dot(left, m_ref[j, : 3 * atoms, w_base:])
        total = high[: 2 * width] + (high[2 * width :] + dot(fhi, m_ref[j, 3 * atoms :, w_base:]))
        cols = total.shape[1] // 2
        hi, lo = split(total)
        for v in range(2):
            rows = slice(v * width, (v + 1) * width)
            for s, ref in enumerate((reach_e_ref, reach_o_ref)):
                cut = slice(s * cols, (s + 1) * cols)
                ref[v, :width, j * cols : (j + 1) * cols] = hi[rows, cut]
                ref[v, width:, j * cols : (j + 1) * cols] = lo[rows, cut]


def partial_kernel(reach_ref, gram_ref, block_ref, *outs, last):
    ext_ref = outs[-1]
    width = block_ref.shape[2]
    bound = (block_ref.shape[1] - 8) // 3
    rows = ext_ref.shape[0] // 3
    used = 3 * bound
    blocks = [block_ref.at[z] for z in range(3)]
    scale_rows(blocks, [ext_ref.at[j * rows : (j + 1) * rows] for j in range(3)], 0)
    if used < rows:
        for j in range(3):
            ext_ref[j * rows + used : (j + 1) * rows] = jnp.zeros((rows - used, 2 * width), BF16)
    grams = []
    for v in range(2):
        both = dot(reach_ref[v], ext_ref[:, v * width : (v + 1) * width])
        grams.append(gram_ref[v] + (both[:width] + both[width:]))
    if last:
        even = lax.rem(lax.axis_index("wide"), 2) == 0
        outs[0][...] = jnp.where(even, grams[0], grams[1])
        outs[1][...] = jnp.where(even, grams[1], grams[0])
    else:
        for v in range(2):
            outs[0][v] = grams[v]


def turn_kernel(m_ref, product_ref, factor_ref, ext_e_ref, ext_o_ref, rotation_ref, out_ref):
    width = factor_ref.shape[2]
    rows = ext_e_ref.shape[0] // 3
    w_base = m_ref.shape[2] - 2 * rows
    exts = []
    for j in range(3):
        part = [ref[j * rows : (j + 1) * rows] for ref in (ext_e_ref, ext_o_ref)]
        exts.append(jnp.concatenate(part, axis=0))
    product = product_ref[...] + apply_rows(m_ref, exts, slice(w_base, None))
    for v in range(2):
        f = jnp.concatenate([factor_ref[v]] * 3, axis=0)
        hi, lo = split(product[:, v * width : (v + 1) * width] * f)
        rhi, rlo = split(rotation_ref[v])
        both = dot(hi, jnp.concatenate([rhi, rlo], axis=1))
        out_ref[v] = both[:, :width] + (both[:, width:] + dot(lo, rhi))


def finish_kernel(
    total_ref, turned_ref, vectors_ref, rotation_ref, *refs, count, own
):
    gram_hbm, out_hbm, gram_scr, out_scr, sems = refs[-5:]
    atoms = vectors_ref.shape[1]
    v = lax.rem(lax.axis_index("wide"), 2)
    v = v if own else 1 - v
    gram = total_ref[...] / count
    gram_scr[...] = gram
    copies = [pltpu.make_async_copy(gram_scr, gram_hbm.at[v], sems.at[0])]
    copies[0].start()
    hi, lo = split(gram)
    rhi, rlo = split(rotation_ref[v])
    step = dot(hi, rhi) + (dot(lo, rhi) + dot(hi, rlo))
    shi, slo = split(step)
    for j in range(3):
        vec = vectors_ref[j]
        turned = turned_ref[v, j * atoms : (j + 1) * atoms]
        out_scr[j] = (turned - (dot(vec, shi) + dot(vec, slo))).astype(BF16)
        copies.append(pltpu.make_async_copy(out_scr.at[j], out_hbm.at[v, j], sems.at[1 + j]))
        copies[-1].start()
    for copy in copies:
        copy.wait()


def swap(array, n_wide, n_narrow, place):
    pairs = []
    for p in range(n_wide):
        for q in range(n_narrow):
            a, b = place(p, q)
            pairs.append((p * n_narrow + q, a * n_narrow + b))
    return lax.ppermute(array, AXES, pairs)


def sum_stages(n_wide, n_narrow):
    bits = [(1 << k, 0) for k in range(1, n_wide.bit_length() - 1)]
    bits += [(0, 1 << k) for k in range(n_narrow.bit_length() - 1)]
    stages = []
    for k in range(0, len(bits), 2):
        steps = bits[k : k + 2]
        if steps[0][0]:
            steps = steps[::-1]
        if len(steps) == 2:
            steps.insert(0, (steps[0][0] ^ steps[1][0], steps[0][1] ^ steps[1][1]))
        stages.append(steps)
    half = len(stages) // 2
    odd = [st[:1] + st[:0:-1] if st[0][1] else st for st in stages[half:] + stages[:half]]
    if any(len(a) != len(b) for a, b in zip(stages, odd)):
        odd = stages
    return [list(zip(a, b)) for a, b in zip(stages, odd)]


def odd_partner(i, n):
    k = i + 1 if i % 2 else i - 1
    return k if 0 <= k < n else None


def call(kernel, out, *args, scratch=(), cost=None, space=VMEM):
    shapes = [jax.ShapeDtypeStruct(s, d) for s, d in out]
    flops, moved = cost or (1000, 1000)
    return pl.pallas_call(
        kernel,
        out_shape=shapes,
        in_specs=[space] * len(args),
        out_specs=[VMEM] * len(shapes),
        scratch_shapes=list(scratch),
        compiler_params=pltpu.CompilerParams(vmem_limit_bytes=24 * 2**20),
        cost_estimate=pl.CostEstimate(flops=flops, bytes_accessed=moved, transcendentals=0),
    )(*args)


def local(vectors, hessian, neighbours, halo_atoms, labels, masses, rotation):
    n_wide = lax.axis_size("wide")
    n_narrow = lax.axis_size("narrow")
    atoms, width = vectors.shape[1:]
    bound = halo_atoms.shape[0]
    slots = hessian.shape[2]
    kpad = -(-slots // 64) * 64
    w_base = -(-(atoms + 3 * bound) // 128) * 128
    w_step = -(-3 * bound // 128) * 128
    w_rows = 2 * w_step

    def exchange(array, place):
        return swap(array, n_wide, n_narrow, place)

    def odd_z(p, q):
        k = odd_partner(q, n_narrow)
        return (p ^ 1, q) if k is None else (p, k)

    def odd_w(p, q):
        k = odd_partner(p, n_wide)
        return (p, q ^ 1) if k is None else (k, q)

    raw = (
        vectors, halo_atoms.reshape(1, bound), labels.reshape(1, atoms), masses, neighbours,
        hessian, rotation,
    )
    hbm = pl.BlockSpec(memory_space=pltpu.HBM)
    rim, vectors, labels, masses, near, hessian, rotation = call(
        prepare_kernel,
        [((3 * bound + 8, width), BF16)] + [(a.shape, a.dtype) for i, a in enumerate(raw) if i != 1],
        *[pltpu.with_memory_space_constraint(a, pltpu.HBM) for a in raw],
        scratch=[pltpu.VMEM((1, bound), I32), pltpu.SemaphoreType.DMA((9,))],
        space=hbm,
    )
    ez = exchange(rim, lambda p, q: (p, q ^ 1))
    oz = exchange(rim, odd_z)

    def build(*refs):
        build_kernel(
            *refs, n_wide=n_wide, n_narrow=n_narrow, bound=bound, w_base=w_base, w_step=w_step
        )

    cost = (9 * atoms * 16 * kpad * (w_base + w_rows), 4 * 2**20)
    (m,) = call(
        build,
        [((3, 6 * atoms, w_base + w_rows), BF16)],
        near, hessian,
        scratch=[
            pltpu.VMEM((kpad, atoms), I32),
            pltpu.VMEM((9, atoms, atoms), BF16),
            pltpu.VMEM((16 * kpad, w_base + w_rows), BF16),
        ],
        cost=cost,
    )
    ez, oz, m = lax.optimization_barrier((ez, oz, m))
    three = jnp.stack([rim, ez, oz])
    ew = exchange(three, lambda p, q: (p ^ 1, q))
    ow = exchange(three, odd_w)
    product, factor, gram, reach_e, reach_o = call(
        local_kernel,
        [
            ((3 * atoms, 2 * width), F32),
            ((2, atoms, width), F32),
            ((2, width, width), F32),
            ((2, 2 * width, 3 * w_step), BF16),
            ((2, 2 * width, 3 * w_step), BF16),
        ],
        m, vectors, labels, masses, rim, ez, oz,
        scratch=[
            pltpu.VMEM((3, w_base, 2 * width), BF16),
            pltpu.VMEM((width, 3 * atoms), F32),
        ],
        cost=cost,
    )
    cost = (12 * width * width * w_rows, 2**20)
    rows = ((3 * w_step, 2 * width), BF16)
    square = ((width, width), F32)
    gram, ext_e = call(
        functools.partial(partial_kernel, last=False),
        [((2, width, width), F32), rows], reach_e, gram, ew, cost=cost,
    )
    mine, other, ext_o = call(
        functools.partial(partial_kernel, last=True),
        [square, square, rows], reach_o, gram, ow, cost=cost,
    )
    (turned,) = call(
        turn_kernel, [((2, 3 * atoms, width), F32)], m, product, factor, ext_e, ext_o, rotation,
        cost=(2 * 18 * atoms * w_rows * 2 * width, 4 * 2**20),
    )
    total = mine + exchange(other, lambda p, q: (p ^ 1, q))
    for k, steps in enumerate(sum_stages(n_wide, n_narrow)):
        parts = [
            exchange(total, lambda p, q, s=s: (p ^ s[p % 2][0], q ^ s[p % 2][1]))
            for s in steps
        ]
        for part in parts:
            total = total + part
        if k == 0:
            total, turned = lax.optimization_barrier((total, turned))
    other = exchange(total, lambda p, q: (p ^ 1, q))
    count = 3.0 * atoms * n_wide * n_narrow
    outs = [
        jax.ShapeDtypeStruct((2, width, width), F32),
        jax.ShapeDtypeStruct((2, 3, atoms, width), BF16),
    ]

    def finish(total, held=()):
        return pl.pallas_call(
            functools.partial(finish_kernel, count=count, own=not held),
            out_shape=outs,
            in_specs=[VMEM] * 4 + [hbm] * len(held),
            out_specs=[hbm] * 2,
            scratch_shapes=[
                pltpu.VMEM((width, width), F32),
                pltpu.VMEM((3, atoms, width), BF16),
                pltpu.SemaphoreType.DMA((4,)),
            ],
            input_output_aliases={4: 0, 5: 1} if held else {},
            compiler_params=pltpu.CompilerParams(vmem_limit_bytes=24 * 2**20),
            cost_estimate=pl.CostEstimate(flops=10**6, bytes_accessed=10**6, transcendentals=0),
        )(total, turned, vectors, rotation, *held)

    return tuple(finish(other, finish(total)))


def solution(mesh):
    n_wide, n_narrow = (mesh.shape[axis] for axis in AXES)
    for size in (n_wide, n_narrow):
        assert size & (size - 1) == 0 and size > 1
    return jax.shard_map(
        local,
        mesh=mesh,
        in_specs=(
            P(None, AXES, None),
            P(None, None, None, AXES),
            P(None, AXES),
            P(AXES),
            P(AXES),
            P(),
            P(),
        ),
        out_specs=(P(), P(None, None, AXES, None)),
        check_vma=False,
    )
```
